256 devices in a mesh: table: 32 (over z, x), scal: 8 (over y, core).
Axes of the slice: x: 4, y: 4, z: 8, core: 2. Of those that a mesh axis runs over, the one named last changes fastest.
Arguments:
- cell_coords: float32 [4, 524288], P(None, ('table', 'scal')), may hold values from 0 to 1
- flamelet_table: float32 [131072, 1024], P('table', 'scal'), may hold values from -15 to 15
- owner_shard: int32 [524288, 1], P(('table', 'scal')), may hold values from 0 to 31; in each aligned block of 64 rows (0 to 63, 64 to 127, ...) at most 5 rows name the same one
- local_bin: int32 [524288], P(('table', 'scal')), may hold values from 0 to 4095
Outputs:
- filtered_fields: float32 [32, 2048, 256], P(None, ('table', 'scal'))
- x_gradient: float32 [32, 2048, 256], P(None, ('table', 'scal'))
The draws below stay inside these ranges and needn't reach their ends.
Inputs may be any that keep to these rules, and one draw needn't show every extreme that they name: `owner_shard`: in each aligned block of 64 rows (one group of one device's cells) no shard is named by more than 5 rows, a bound that some block reaches.
All inputs are finite; a program needn't handle non-finite values.
Results may differ from the reference program's by a relative error of at most 0.00012.
Values sent between devices are 32-bit elements; how exact they have to be, the bound alone decides.
A program may use at most 128 MiB of HBM per device.

```python
import math
import jax
import jax.numpy as jnp
import numpy as np
from jax import lax

SCAL_ALL = 32
K = 32
BINS_DEV = 4096
BX = 8
LG = 8
NX = 256
LINES = 2048
CELL_DEV = 2048
CELLS = 524288
MOST = 5
N_TABLE = 32
N_SCAL = 8


def with_ends(entries, rng, smallest, top_value):
    longest = entries.shape.index(max(entries.shape))
    spots = []
    for shift in (0, 1):
        where = [jax.random.randint(jax.random.fold_in(rng, axis), (), 0, length) for axis, length in enumerate(entries.shape)]
        where[longest] = (where[longest] + shift) % entries.shape[longest]
        spots.append(tuple(where))
    return entries.at[spots[0]].set(smallest).at[spots[1]].set(top_value)


def level_of(rng, shape, cuts, smallest, top_value):
    gain, own = 1.0, jax.random.fold_in(rng, 6)
    for axis_at, shards_of in cuts:
        draws = jnp.exp(jax.random.uniform(jax.random.fold_in(own, axis_at), (shards_of,), jnp.float32, smallest / len(cuts), top_value / len(cuts)))
        gain = gain * jnp.repeat(draws, shape[axis_at] // shards_of).reshape([-1 if axis == axis_at else 1 for axis in range(len(shape))])
    return gain


def shared_out(own_key, own, number, rows, count, top, limit, slope):
    ranking = jax.random.permutation(own_key, count)
    crowded, common = portions_of(count, rows * top, limit, slope, True), portions_of(count, rows * top, limit, slope, False)
    places = jnp.arange(count)

    def named(tallies, turn):
        used = int((tallies > 0).sum())
        fixed = max(1, used // 4)
        passed = fixed + (places - fixed + turn * (used - fixed)) % max(1, count - fixed)
        return jnp.zeros((count,), jnp.int32).at[ranking[jnp.where(places < fixed, places, passed)]].set(jnp.asarray(tallies, jnp.int32))

    tallies = jnp.where(number % 4 == 0, named(crowded, number // 4), named(common, number - number // 4 - 1))
    mixed = jax.random.permutation(jax.random.fold_in(own, 3), count)
    source_of, sink = mixed[0:count // 2 * 2:2], mixed[1:count // 2 * 2:2]
    slack = jnp.minimum(tallies[source_of] - 1, limit - tallies[sink]) // 2
    slack = jnp.where((source_of == ranking[0]) | (sink == ranking[0]) | (tallies[sink] == 0), 0, jnp.maximum(slack, 0))
    passed = jax.random.randint(jax.random.fold_in(own, 4), (count // 2,), 0, 1 << 20) % (slack + 1)
    tallies = tallies.at[source_of].add(-passed).at[sink].add(passed)
    labels = jnp.searchsorted(jnp.cumsum(tallies), jnp.arange(rows * top), side="right").astype(jnp.int32)
    grid = labels.reshape(top, rows).T
    grid = grid[jax.random.permutation(jax.random.fold_in(own, 1), rows)]
    turn = jax.random.randint(jax.random.fold_in(own, 2), (rows, 1), 0, top)
    return jnp.take_along_axis(grid, (jnp.arange(top)[None, :] + turn) % top, axis=1)


def portions_of(number_of, total, bound, lean, full):
    portions = [(1 << 20) // math.isqrt(grade ** lean) + 1 for grade in range(1, number_of + 1)]
    largest = bound if full else min(bound, max(-(-total // number_of), total * portions[0] // sum(portions)))
    least = 1 if total - largest >= number_of - 1 else 0
    counts, spare = [largest] + [least] * (number_of - 1), total - largest - least * (number_of - 1)
    while spare > 0:
        free = [i for i in range(1, number_of) if counts[i] < largest] or [i for i in range(1, number_of) if counts[i] < bound]
        pool, budget = sum([portions[i] for i in free]), spare
        for i in free:
            extra = min(bound - counts[i], max(1, budget * portions[i] // pool), spare)
            counts[i] = counts[i] + extra
            spare = spare - extra
    return np.array(counts)


def gaussian(rng, extent, spread, bound, pieces=(), held_as=jnp.bfloat16):
    array = spread * jax.random.normal(rng, extent, jnp.float32)
    if pieces:
        array = array * level_of(rng, extent, pieces, -0.22, 0.18)
    return jnp.clip(array, -bound, bound).astype(held_as)


def setup_inputs(seed: int = 0) -> dict:
    arg_keys = jax.random.split(jax.random.key(seed), 5)
    cell_coords = jnp.clip(1.0 * jax.random.uniform(arg_keys[0], (4, CELLS), jnp.float32) ** level_of(arg_keys[0], (4, CELLS), ((1, 256),), -0.2, 0.2), 0.0, 1.0)
    flamelet_table = gaussian(arg_keys[1], (N_TABLE * BINS_DEV, SCAL_ALL * K), 2.5, 15.0, ((0, 32), (1, 8)), jnp.float32)
    owner_shard_keys = jax.random.split(jax.random.fold_in(arg_keys[2], 1), CELLS // (BX * LG))
    owner_shard_turns = jax.random.permutation(jax.random.fold_in(arg_keys[2], 3), CELLS // (BX * LG))
    owner_shard = jax.vmap(lambda own, number: shared_out(jax.random.fold_in(arg_keys[2], 2), own, number, BX * LG, N_TABLE, 1, MOST, 2))(owner_shard_keys, owner_shard_turns).reshape((CELLS, 1))
    local_bin = with_ends(jax.random.randint(arg_keys[3], (CELLS,), 0, BINS_DEV), jax.random.fold_in(arg_keys[3], 1), 0, BINS_DEV - 1).astype(jnp.int32)
    return {"cell_coords": cell_coords, "flamelet_table": flamelet_table, "owner_shard": owner_shard, "local_bin": local_bin}


strength = 0.499

def spline_weights(coords):
    linear = [jnp.stack([1.0 - coords[axis_id], coords[axis_id]]) for axis_id in range(3)]
    frac_last = coords[3]
    square = frac_last * frac_last
    cube = square * frac_last
    remain = 1.0 - frac_last
    cubic = jnp.stack([remain * remain * remain / 6.0, (3.0 * cube - 6.0 * square + 4.0) / 6.0, (-3.0 * cube + 3.0 * square + 3.0 * frac_last + 1.0) / 6.0, cube / 6.0])
    product = linear[0][:, None, None, None, :] * linear[1][None, :, None, None, :] * linear[2][None, None, :, None, :] * cubic[None, None, None, :, :]
    return product.reshape(-1, coords.shape[1])

def filter_matrix(length):
    positions = jnp.arange(length)
    offset = positions[None, :] - positions[:, None]
    distance = jnp.abs(offset)
    interior = (positions >= 3) & (positions <= length - 4)
    coeffs = [(11.0 + 10.0 * strength) / 16.0, (15.0 + 34.0 * strength) / 64.0, (-3.0 + 6.0 * strength) / 32.0, (1.0 - 2.0 * strength) / 64.0]
    band = jnp.zeros((length, length), jnp.float32)
    for reach in range(4):
        band = band + jnp.where(distance == reach, coeffs[reach], 0.0).astype(jnp.float32)
    right_side = jnp.where(interior[:, None], band, (offset == 0).astype(jnp.float32))
    coupling = jnp.where(interior, strength, 0.0).astype(jnp.float32)
    main_diag = jnp.ones((length,), jnp.float32)
    return lax.linalg.tridiagonal_solve(coupling, main_diag, coupling, right_side)

def derivative_matrix(length):
    positions = jnp.arange(length)
    offset = positions[None, :] - positions[:, None]
    distance = jnp.abs(offset)
    direction = jnp.sign(offset).astype(jnp.float32)
    boundary = (positions == 0) | (positions == length - 1)
    second = (positions == 1) | (positions == length - 2)
    interior = jnp.logical_not(boundary | second)
    below_diag = jnp.where(interior, 1.0 / 3.0, jnp.where(second, 0.25, jnp.where(positions == length - 1, 2.0, 0.0))).astype(jnp.float32)
    above_diag = jnp.where(interior, 1.0 / 3.0, jnp.where(second, 0.25, jnp.where(positions == 0, 2.0, 0.0))).astype(jnp.float32)
    inner_rows = direction * (jnp.where(distance == 1, 7.0 / 9.0, 0.0) + jnp.where(distance == 2, 1.0 / 36.0, 0.0))
    second_rows = direction * jnp.where(distance == 1, 0.75, 0.0)
    first_row = jnp.where(offset == 0, -2.5, jnp.where(offset == 1, 2.0, jnp.where(offset == 2, 0.5, 0.0)))
    final_row = jnp.where(offset == 0, 2.5, jnp.where(offset == -1, -2.0, jnp.where(offset == -2, -0.5, 0.0)))
    right_side = jnp.where(interior[:, None], inner_rows, jnp.where(second[:, None], second_rows, jnp.where((positions == 0)[:, None], first_row, final_row))).astype(jnp.float32)
    main_diag = jnp.ones((length,), jnp.float32)
    return lax.linalg.tridiagonal_solve(below_diag, main_diag, above_diag, right_side)

def reference(cell_coords, flamelet_table, owner_shard, local_bin):
    row_index = (owner_shard[:, 0] * BINS_DEV + local_bin).astype(jnp.int32)
    block_count = row_index.shape[0] // CELL_DEV

    def one_block(inputs):
        coords, wanted = inputs
        weights = spline_weights(coords)
        gathered = jnp.take(flamelet_table, wanted, axis=0).reshape(CELL_DEV, SCAL_ALL, K)
        return jnp.einsum('nsk,kn->sn', gathered, weights, precision=lax.Precision.HIGHEST)
    looked = lax.map(one_block, (cell_coords.reshape(4, block_count, CELL_DEV).transpose(1, 0, 2), row_index.reshape(block_count, CELL_DEV)))
    looked = looked.transpose(1, 0, 2).reshape(SCAL_ALL, N_TABLE, N_SCAL, N_TABLE, LG, BX)
    gridded = looked.transpose(0, 3, 2, 4, 1, 5).reshape(SCAL_ALL * LINES, NX)
    filtered = jnp.dot(gridded, filter_matrix(NX).T, precision=lax.Precision.HIGHEST)
    gradient = jnp.dot(filtered, derivative_matrix(NX).T, precision=lax.Precision.HIGHEST)
    return (filtered.reshape(SCAL_ALL, LINES, NX), gradient.reshape(SCAL_ALL, LINES, NX))
```

```python
import functools

import jax
import jax.numpy as jnp
import numpy as np
from jax import lax
from jax.experimental import pallas as pl
from jax.experimental.pallas import tpu as pltpu
from jax.sharding import PartitionSpec as P

F32, BF16, I32 = jnp.float32, jnp.bfloat16, jnp.int32
MESH = pl.DeviceIdType.MESH

strength = 0.499


def thomas_solve(below, middle, above, right_side):
    length = middle.shape[0]
    upper_factor = np.zeros(length)
    solved = np.zeros(right_side.shape)
    for row in range(length):
        if row == 0:
            denom = middle[0]
            solved[0] = right_side[0] / denom
        else:
            denom = middle[row] - below[row] * upper_factor[row - 1]
            solved[row] = (right_side[row] - below[row] * solved[row - 1]) / denom
        upper_factor[row] = above[row] / denom
    for row in range(length - 2, -1, -1):
        solved[row] = solved[row] - upper_factor[row] * solved[row + 1]
    return solved


def filter_table(length):
    positions = np.arange(length)
    offset = positions[None, :] - positions[:, None]
    distance = np.abs(offset)
    interior = (positions >= 3) & (positions <= length - 4)
    coeffs = [
        (11.0 + 10.0 * strength) / 16.0,
        (15.0 + 34.0 * strength) / 64.0,
        (-3.0 + 6.0 * strength) / 32.0,
        (1.0 - 2.0 * strength) / 64.0,
    ]
    band = np.zeros((length, length))
    for reach in range(4):
        band = band + np.where(distance == reach, coeffs[reach], 0.0)
    right_side = np.where(interior[:, None], band, np.where(offset == 0, 1.0, 0.0))
    coupling = np.where(interior, strength, 0.0)
    return thomas_solve(coupling, np.ones(length), coupling, right_side)


def derivative_table(length):
    positions = np.arange(length)
    offset = positions[None, :] - positions[:, None]
    distance = np.abs(offset)
    direction = np.sign(offset) * 1.0
    boundary = (positions == 0) | (positions == length - 1)
    second = (positions == 1) | (positions == length - 2)
    interior = ~(boundary | second)
    below_diag = np.where(
        interior, 1.0 / 3.0, np.where(second, 0.25, np.where(positions == length - 1, 2.0, 0.0))
    )
    above_diag = np.where(
        interior, 1.0 / 3.0, np.where(second, 0.25, np.where(positions == 0, 2.0, 0.0))
    )
    inner_rows = direction * (
        np.where(distance == 1, 7.0 / 9.0, 0.0) + np.where(distance == 2, 1.0 / 36.0, 0.0)
    )
    second_rows = direction * np.where(distance == 1, 0.75, 0.0)
    first_row = np.where(
        offset == 0, -2.5, np.where(offset == 1, 2.0, np.where(offset == 2, 0.5, 0.0))
    )
    final_row = np.where(
        offset == 0, 2.5, np.where(offset == -1, -2.0, np.where(offset == -2, -0.5, 0.0))
    )
    right_side = np.where(
        interior[:, None],
        inner_rows,
        np.where(
            second[:, None], second_rows, np.where((positions == 0)[:, None], first_row, final_row)
        ),
    )
    return thomas_solve(below_diag, np.ones(length), above_diag, right_side)


NT = (((1,), (1,)), ((), ()))
TN = (((0,), (0,)), ((), ()))
TABLES = 32
YS = 4
MOST = 5


def split3(x):
    hi = x.astype(BF16).astype(F32)
    rest = x - hi
    mid = rest.astype(BF16).astype(F32)
    return hi, mid, rest - mid


def iota(shape, axis):
    return lax.broadcasted_iota(I32, shape, axis)


def request_kernel(coords_ref, owner_ref, bin_ref, msg_ref, pay_ref, acc5, acc6, acc7):
    pay_ref[0:1, :] = bin_ref[...].astype(F32)
    pay_ref[1:5, :] = coords_ref[...]
    pay_ref[5:8, :] = jnp.zeros((3, pay_ref.shape[1]), F32)
    width = 256
    at, to = iota((width, width), 0), iota((width, width), 1)
    before = jnp.where((at < to) & ((at >> 6) == (to >> 6)), 1.0, 0.0).astype(BF16)
    msg_ref[...] = jnp.zeros_like(msg_ref)
    acc5[...] = jnp.zeros_like(acc5)
    acc6[...] = jnp.zeros_like(acc6)
    acc7[...] = jnp.zeros_like(acc7)

    def chunk(step, carry):
        lanes = pl.ds(pl.multiple_of(step * width, width), width)
        owner = owner_ref[:, lanes]
        pay = pay_ref[:, lanes]
        hit = iota((TABLES, width), 0) == owner
        ones = jnp.where(hit, 1.0, 0.0).astype(BF16)
        ahead = jnp.dot(ones, before, preferred_element_type=F32)
        rank = jnp.sum(jnp.where(hit, ahead, 0.0), axis=0, keepdims=True).astype(I32)
        group = step * (width // 64) + (iota((1, width), 1) >> 6)
        slot = rank * 32 + group
        place = jnp.where(iota((128, width), 0) == slot, 1.0, 0.0).astype(BF16)
        last = jnp.where(hit & (rank == MOST - 1), 1.0, 0.0).astype(BF16)
        mine = iota((TABLES, 8, width), 0) == jnp.broadcast_to(owner[None], (TABLES, 8, width))
        same = (iota((128, width), 0) & 31) == group
        for part in split3(pay):
            left = jnp.where(mine, part[None], 0.0).reshape(TABLES * 8, width).astype(BF16)
            msg_ref[...] += lax.dot_general(left, place, NT, preferred_element_type=F32)
            fields = jnp.concatenate(
                [jnp.broadcast_to(part[f : f + 1], (32, width)) for f in range(4)], axis=0
            )
            right = jnp.where(same, fields, 0.0).astype(BF16)
            acc5[...] += lax.dot_general(last, right, NT, preferred_element_type=F32)
            field = jnp.where(same & (iota((128, width), 0) < 32), part[4:5], 0.0).astype(BF16)
            acc6[...] += lax.dot_general(last, field, NT, preferred_element_type=F32)
        code = (owner * 8 + rank).astype(F32)
        own = jnp.where(iota((TABLES, width), 0) == group, code, 0.0).astype(BF16)
        spot = jnp.where(
            iota((128, width), 0) == (iota((128, width), 1) & 63), 1.0, 0.0
        ).astype(BF16)
        acc7[...] += lax.dot_general(own, spot, NT, preferred_element_type=F32)
        return carry

    lax.fori_loop(0, owner_ref.shape[1] // width, chunk, 0)
    msg_ref[pl.ds(5, TABLES, stride=8), :] = acc5[...]
    msg_ref[pl.ds(6, TABLES, stride=8), :] = acc6[...]
    msg_ref[pl.ds(7, TABLES, stride=8), :] = acc7[...]


def enter(me_t, me_s, with_partner):
    barrier = pltpu.get_barrier_semaphore()

    def greet(step, carry):
        pl.semaphore_signal(
            barrier, inc=1, device_id=(lax.rem(me_t + step, TABLES), me_s), device_id_type=MESH
        )
        return carry

    lax.fori_loop(1, TABLES, greet, 0)
    for step in range(1, YS):
        pl.semaphore_signal(
            barrier, inc=1, device_id=(me_t, lax.rem(me_s + 2 * step, 2 * YS)), device_id_type=MESH
        )
    if with_partner:
        core = lax.rem(me_s, 2)
        pl.semaphore_signal(
            barrier, inc=1, device_id=(me_t, me_s + 1 - 2 * core), device_id_type=MESH
        )
    pl.semaphore_wait(barrier, TABLES - 1 + YS - 1 + (1 if with_partner else 0))


def far_and_near(body):
    def pair(step, carry):
        body(step)
        body(TABLES - step)
        return carry

    lax.fori_loop(1, TABLES // 2, pair, 0)
    body(TABLES // 2)


def exchange_kernel(
    msg_ref, table_ref, got_ref, all_ref, other_ref, local_sem, swap_sem, row_sem, y_send, y_recv
):
    me_t, me_s = lax.axis_index("table"), lax.axis_index("scal")
    core = lax.rem(me_s, 2)
    me_y = lax.div(me_s, 2)
    partner = (me_t, me_s + 1 - 2 * core)
    enter(me_t, me_s, True)
    swap = pltpu.make_async_remote_copy(
        table_ref, other_ref, swap_sem.at[0], swap_sem.at[1], device_id=partner, device_id_type=MESH
    )

    def send(step):
        to = lax.rem(me_t + step, TABLES)
        pltpu.make_async_remote_copy(
            msg_ref.at[to], got_ref.at[me_t], row_sem.at[0], row_sem.at[1],
            device_id=(to, me_s), device_id_type=MESH,
        ).start()

    far_and_near(send)
    own = pltpu.make_async_copy(msg_ref.at[me_t], got_ref.at[me_t], local_sem.at[0])
    own.start()
    swap.start()
    own.wait()
    whole = pltpu.make_async_remote_copy(
        msg_ref.at[pl.ds(0, TABLES - 1)], got_ref.at[pl.ds(0, TABLES - 1)],
        row_sem.at[0], row_sem.at[1], device_id=partner, device_id_type=MESH,
    )
    whole.wait_recv()
    copies = []
    for step in range(1, YS):
        to = lax.rem(me_s + 2 * step, 2 * YS)
        copy = pltpu.make_async_remote_copy(
            got_ref, all_ref.at[me_y], y_send.at[step - 1], y_recv.at[step - 1],
            device_id=(me_t, to), device_id_type=MESH,
        )
        copy.start()
        copies.append(copy)
    keep = pltpu.make_async_copy(got_ref, all_ref.at[me_y], local_sem.at[1])
    keep.start()
    whole.wait_send()
    keep.wait()
    for copy in copies:
        copy.wait()
    swap.wait()


def lookup_kernel(idx_ref, req_ref, near_ref, far_ref, out_ref, near, far, rows0, rows1, acc, pick, sem):
    loads = [
        pltpu.make_async_copy(near_ref, near, sem.at[0]),
        pltpu.make_async_copy(far_ref, far, sem.at[1]),
    ]
    for load in loads:
        load.start()
    core = lax.rem(lax.axis_index("scal"), 2)
    slots = 32 * MOST
    k, lane = iota((256, 128), 0), iota((256, 128), 1)
    half = jnp.where((k >> 7) == 0, core, 1 - core)
    base = half * 4 + ((k >> 5) & 3)
    for b in range(16):
        pick[b] = jnp.where(lane == base + 8 * b, 1.0, 0.0).astype(BF16)
    for load in loads:
        load.wait()
    spread = jnp.where((iota((96, 128), 0) & 31) == (iota((96, 128), 1) & 31), 1.0, 0.0).astype(BF16)
    kk = iota((32, 256), 0)

    def block(b, base_block):
        blk = base_block + b
        for i in range(slots):
            row = idx_ref[2 * blk + (i // 128), i % 128]
            rows0[i : i + 1, :] = near[pl.ds(row, 1), :]
            rows1[i : i + 1, :] = far[pl.ds(row, 1), :]
        tile = req_ref[blk]
        tail = tile[5:6]
        f = [
            jnp.concatenate([tile[1 + n : 2 + n], extra], axis=1)
            for n, extra in enumerate(
                (pltpu.roll(tail, 96, 1), pltpu.roll(tail, 64, 1), pltpu.roll(tail, 32, 1), tile[6:7])
            )
        ]
        lin = [
            jnp.where(((kk >> bit) & 1) == 0, 1.0 - f[n], f[n]) for n, bit in enumerate((4, 3, 2))
        ]
        last = f[3]
        square = last * last
        cube = square * last
        remain = 1.0 - last
        cubic = (
            remain * remain * remain * (1.0 / 6.0),
            (3.0 * cube - 6.0 * square + 4.0) * (1.0 / 6.0),
            (-3.0 * cube + 3.0 * square + 3.0 * last + 1.0) * (1.0 / 6.0),
            cube * (1.0 / 6.0),
        )
        d = kk & 3
        bent = jnp.where(
            d < 2, jnp.where(d == 0, cubic[0], cubic[1]), jnp.where(d == 2, cubic[2], cubic[3])
        )
        weight = lin[0] * lin[1] * lin[2] * bent
        parts = jnp.concatenate([part.astype(BF16) for part in split3(weight)], axis=0)
        wide = lax.dot_general(parts[:, :slots], spread, TN, preferred_element_type=F32)
        left, right = rows0[...] * wide, rows1[...] * wide
        left_hi, right_hi = left.astype(BF16), right.astype(BF16)
        left_lo = (left - left_hi.astype(F32)).astype(BF16)
        right_lo = (right - right_hi.astype(F32)).astype(BF16)
        chosen = pick[b]
        acc[...] += jnp.dot(
            jnp.concatenate([left_hi, right_hi], axis=1), chosen, preferred_element_type=F32
        ) + jnp.dot(jnp.concatenate([left_lo, right_lo], axis=1), chosen, preferred_element_type=F32)
        return base_block

    def section(step, carry):
        acc[...] = jnp.zeros_like(acc)
        lax.fori_loop(0, 16, block, step * 16)
        y, half_t = step // 2, lax.rem(step, 2)
        for q in range(MOST):
            for g in range(32):
                out_ref[y, g, half_t, q : q + 1, :] = acc[q * 32 + g : q * 32 + g + 1, :]
        return carry

    lax.fori_loop(0, 2 * YS, section, 0)


def reply_kernel(out_ref, got_ref, mid_ref, y_send, y_recv, row_sem, local_sem):
    me_t, me_s = lax.axis_index("table"), lax.axis_index("scal")
    me_y = lax.div(me_s, 2)
    enter(me_t, me_s, False)
    copies = []
    for step in range(1, YS):
        to_y = lax.rem(me_y + step, YS)
        copy = pltpu.make_async_remote_copy(
            out_ref.at[to_y], mid_ref.at[me_y], y_send.at[step - 1], y_recv.at[step - 1],
            device_id=(me_t, lax.rem(me_s + 2 * step, 2 * YS)), device_id_type=MESH,
        )
        copy.start()
        copies.append(copy)

    def pass_on(source, y):
        def send(step):
            to = lax.rem(me_t + step, TABLES)
            pltpu.make_async_remote_copy(
                source.at[to], got_ref.at[me_t, y], row_sem.at[0], row_sem.at[1],
                device_id=(to, me_s), device_id_type=MESH,
            ).start()

        far_and_near(send)

    keeps = [pltpu.make_async_copy(out_ref.at[me_y, me_t], got_ref.at[me_t, me_y], local_sem.at[0])]
    keeps[0].start()
    pass_on(out_ref.at[me_y], me_y)
    for step in range(1, YS):
        copies[step - 1].wait_recv()
        y = lax.rem(me_y + YS - step, YS)
        pass_on(mid_ref.at[y], y)
        keep = pltpu.make_async_copy(mid_ref.at[y, me_t], got_ref.at[me_t, y], local_sem.at[step])
        keep.start()
        keeps.append(keep)
    for keep in keeps:
        keep.wait()
    for copy in copies:
        copy.wait_send()
    whole = pltpu.make_async_remote_copy(
        got_ref.at[pl.ds(0, TABLES - 1)], got_ref.at[pl.ds(0, TABLES - 1)],
        row_sem.at[0], row_sem.at[1],
        device_id=(me_t, lax.rem(me_s + 2, 2 * YS)), device_id_type=MESH,
    )
    whole.wait_send()
    whole.wait_recv()


def filter_kernel(got_ref, code_ref, ops_ref, fil_ref, grad_ref, flat, turned, pencil):
    for y in range(YS):
        for half_t in range(2):
            at = 2 * y + half_t
            for o in range(TABLES):
                flat[at, o * 8 : o * 8 + MOST, :] = got_ref[o, y, half_t]
            turned[at] = flat[at].T

    lane = iota((8, 128), 1)

    def line_block(half_t):
        for y in range(YS):
            at = 2 * y + half_t
            sums = [jnp.zeros((8, 128), F32) for _ in range(8)]
            for b in range(16):
                code = code_ref[half_t * 16 + b, 7:8, :].astype(I32)
                code = jnp.broadcast_to(code, (8, 128))
                low = code & 127
                near = jnp.take_along_axis(turned[at, b * 8 : b * 8 + 8, 0:128], low, axis=1)
                far = jnp.take_along_axis(turned[at, b * 8 : b * 8 + 8, 128:256], low, axis=1)
                cells = jnp.where(code < 128, near, far)
                for r in range(8):
                    moved = pltpu.roll(cells, ((b - r) * 8) % 128, 1)
                    sums[r] = jnp.where((lane >> 3) == b, moved, sums[r])
            for r in range(8):
                pencil[half_t, pl.ds(y * 64 + r, 8, stride=8), :] = sums[r]

    line_block(0)
    line_block(1)
    values = jnp.concatenate([pencil[0], pencil[1]], axis=1)
    fil_ref[...] = jnp.dot(
        values, ops_ref[:, 0:256], precision=lax.Precision.HIGHEST, preferred_element_type=F32
    )
    grad_ref[...] = jnp.dot(
        values, ops_ref[:, 256:512], precision=lax.Precision.HIGHEST, preferred_element_type=F32
    )


def on_device(cell_coords, flamelet_table, owner_shard, local_bin):
    cells = cell_coords.shape[1]
    bins = flamelet_table.shape[0]
    dma = pltpu.SemaphoreType.DMA
    vmem = pl.BlockSpec(memory_space=pltpu.VMEM)
    anywhere = pl.BlockSpec(memory_space=pl.ANY)
    shape = jax.ShapeDtypeStruct
    msg = pl.pallas_call(
        request_kernel,
        out_shape=shape((TABLES * 8, 128), F32),
        in_specs=[vmem] * 3,
        out_specs=vmem,
        scratch_shapes=[
            pltpu.VMEM((8, cells), F32),
            pltpu.VMEM((TABLES, 128), F32),
            pltpu.VMEM((TABLES, 128), F32),
            pltpu.VMEM((TABLES, 128), F32),
        ],
        name="build_requests",
    )(cell_coords, owner_shard.T, local_bin.reshape(1, cells))
    got, everything, other = pl.pallas_call(
        exchange_kernel,
        out_shape=(
            shape((TABLES, 8, 128), F32),
            shape((YS, TABLES, 8, 128), F32),
            shape((bins, 128), F32),
        ),
        in_specs=[anywhere] * 2,
        out_specs=(anywhere,) * 3,
        scratch_shapes=[dma((2,)), dma((2,)), dma((2,)), dma((YS - 1,)), dma((YS - 1,))],
        compiler_params=pltpu.CompilerParams(collective_id=0, has_side_effects=True),
        name="exchange_requests",
    )(msg.reshape(TABLES, 8, 128), flamelet_table)
    rows = everything.reshape(YS * TABLES, 8, 128)
    index = jnp.stack([rows[:, 0], rows[:, 5]], axis=1).astype(I32).reshape(2 * YS * TABLES, 128)
    out = pl.pallas_call(
        lookup_kernel,
        out_shape=shape((YS, TABLES, 2, MOST, 128), F32),
        in_specs=[pl.BlockSpec(memory_space=pltpu.SMEM), vmem, anywhere, anywhere],
        out_specs=vmem,
        scratch_shapes=[
            pltpu.VMEM((bins, 128), F32),
            pltpu.VMEM((bins, 128), F32),
            pltpu.VMEM((32 * MOST, 128), F32),
            pltpu.VMEM((32 * MOST, 128), F32),
            pltpu.VMEM((32 * MOST, 128), F32),
            pltpu.VMEM((16, 256, 128), BF16),
            dma((2,)),
        ],
        name="look_up",
    )(index, rows, flamelet_table, other)
    back, _ = pl.pallas_call(
        reply_kernel,
        out_shape=(
            shape((TABLES, YS, 2, MOST, 128), F32),
            shape((YS, TABLES, 2, MOST, 128), F32),
        ),
        in_specs=[anywhere],
        out_specs=(anywhere,) * 2,
        scratch_shapes=[dma((YS - 1,)), dma((YS - 1,)), dma((2,)), dma((YS,))],
        compiler_params=pltpu.CompilerParams(collective_id=1, has_side_effects=True),
        name="send_replies",
    )(out)
    length = 8 * TABLES
    filter_op = filter_table(length)
    ops = np.concatenate([filter_op.T, (derivative_table(length) @ filter_op).T], axis=1)
    filtered, gradient = pl.pallas_call(
        filter_kernel,
        out_shape=(shape((256, length), F32), shape((256, length), F32)),
        in_specs=[vmem] * 3,
        out_specs=(vmem,) * 2,
        scratch_shapes=[
            pltpu.VMEM((2 * YS, 256, 128), F32),
            pltpu.VMEM((2 * YS, 128, 256), F32),
            pltpu.VMEM((2, 256, 128), F32),
        ],
        name="place_and_filter",
    )(back, got, jnp.asarray(ops.astype(np.float32)))
    return filtered.reshape(32, 8, length), gradient.reshape(32, 8, length)


def solution(mesh):
    return jax.shard_map(
        on_device,
        mesh=mesh,
        in_specs=(
            P(None, ("table", "scal")),
            P("table", "scal"),
            P(("table", "scal"), None),
            P(("table", "scal")),
        ),
        out_specs=(P(None, ("table", "scal"), None), P(None, ("table", "scal"), None)),
        check_vma=False,
    )
```

```python
import functools

import jax
import jax.numpy as jnp
import numpy as np
from jax import lax
from jax.experimental import pallas as pl
from jax.experimental.pallas import tpu as pltpu
from jax.sharding import PartitionSpec as P

F32, BF16, I32 = jnp.float32, jnp.bfloat16, jnp.int32
MESH = pl.DeviceIdType.MESH

strength = 0.499


def thomas_solve(below, middle, above, right_side):
    length = middle.shape[0]
    upper_factor = np.zeros(length)
    solved = np.zeros(right_side.shape)
    for row in range(length):
        if row == 0:
            denom = middle[0]
            solved[0] = right_side[0] / denom
        else:
            denom = middle[row] - below[row] * upper_factor[row - 1]
            solved[row] = (right_side[row] - below[row] * solved[row - 1]) / denom
        upper_factor[row] = above[row] / denom
    for row in range(length - 2, -1, -1):
        solved[row] = solved[row] - upper_factor[row] * solved[row + 1]
    return solved


def filter_table(length):
    positions = np.arange(length)
    offset = positions[None, :] - positions[:, None]
    distance = np.abs(offset)
    interior = (positions >= 3) & (positions <= length - 4)
    coeffs = [
        (11.0 + 10.0 * strength) / 16.0,
        (15.0 + 34.0 * strength) / 64.0,
        (-3.0 + 6.0 * strength) / 32.0,
        (1.0 - 2.0 * strength) / 64.0,
    ]
    band = np.zeros((length, length))
    for reach in range(4):
        band = band + np.where(distance == reach, coeffs[reach], 0.0)
    right_side = np.where(interior[:, None], band, np.where(offset == 0, 1.0, 0.0))
    coupling = np.where(interior, strength, 0.0)
    return thomas_solve(coupling, np.ones(length), coupling, right_side)


def derivative_table(length):
    positions = np.arange(length)
    offset = positions[None, :] - positions[:, None]
    distance = np.abs(offset)
    direction = np.sign(offset) * 1.0
    boundary = (positions == 0) | (positions == length - 1)
    second = (positions == 1) | (positions == length - 2)
    interior = ~(boundary | second)
    below_diag = np.where(
        interior, 1.0 / 3.0, np.where(second, 0.25, np.where(positions == length - 1, 2.0, 0.0))
    )
    above_diag = np.where(
        interior, 1.0 / 3.0, np.where(second, 0.25, np.where(positions == 0, 2.0, 0.0))
    )
    inner_rows = direction * (
        np.where(distance == 1, 7.0 / 9.0, 0.0) + np.where(distance == 2, 1.0 / 36.0, 0.0)
    )
    second_rows = direction * np.where(distance == 1, 0.75, 0.0)
    first_row = np.where(
        offset == 0, -2.5, np.where(offset == 1, 2.0, np.where(offset == 2, 0.5, 0.0))
    )
    final_row = np.where(
        offset == 0, 2.5, np.where(offset == -1, -2.0, np.where(offset == -2, -0.5, 0.0))
    )
    right_side = np.where(
        interior[:, None],
        inner_rows,
        np.where(
            second[:, None], second_rows, np.where((positions == 0)[:, None], first_row, final_row)
        ),
    )
    return thomas_solve(below_diag, np.ones(length), above_diag, right_side)


NT = (((1,), (1,)), ((), ()))
TN = (((0,), (0,)), ((), ()))
TABLES = 32
YS = 4
MOST = 5


def split3(x):
    hi = x.astype(BF16).astype(F32)
    rest = x - hi
    mid = rest.astype(BF16).astype(F32)
    return hi, mid, rest - mid


def iota(shape, axis):
    return lax.broadcasted_iota(I32, shape, axis)


def request_kernel(coords_ref, owner_ref, bin_ref, msg_ref, pay_ref, acc5, acc6, acc7):
    pay_ref[0:1, :] = bin_ref[...].astype(F32)
    pay_ref[1:5, :] = coords_ref[...]
    pay_ref[5:8, :] = jnp.zeros((3, pay_ref.shape[1]), F32)
    width = 256
    at, to = iota((width, width), 0), iota((width, width), 1)
    before = jnp.where((at < to) & ((at >> 6) == (to >> 6)), 1.0, 0.0).astype(BF16)
    msg_ref[...] = jnp.zeros_like(msg_ref)
    acc5[...] = jnp.zeros_like(acc5)
    acc6[...] = jnp.zeros_like(acc6)
    acc7[...] = jnp.zeros_like(acc7)

    def chunk(step, carry):
        lanes = pl.ds(pl.multiple_of(step * width, width), width)
        owner = owner_ref[:, lanes]
        pay = pay_ref[:, lanes]
        hit = iota((TABLES, width), 0) == owner
        ones = jnp.where(hit, 1.0, 0.0).astype(BF16)
        ahead = jnp.dot(ones, before, preferred_element_type=F32)
        rank = jnp.sum(jnp.where(hit, ahead, 0.0), axis=0, keepdims=True).astype(I32)
        group = step * (width // 64) + (iota((1, width), 1) >> 6)
        slot = rank * 32 + group
        place = jnp.where(iota((128, width), 0) == slot, 1.0, 0.0).astype(BF16)
        last = jnp.where(hit & (rank == MOST - 1), 1.0, 0.0).astype(BF16)
        mine = iota((TABLES, 8, width), 0) == jnp.broadcast_to(owner[None], (TABLES, 8, width))
        same = (iota((128, width), 0) & 31) == group
        for part in split3(pay):
            left = jnp.where(mine, part[None], 0.0).reshape(TABLES * 8, width).astype(BF16)
            msg_ref[...] += lax.dot_general(left, place, NT, preferred_element_type=F32)
            fields = jnp.concatenate(
                [jnp.broadcast_to(part[f : f + 1], (32, width)) for f in range(4)], axis=0
            )
            right = jnp.where(same, fields, 0.0).astype(BF16)
            acc5[...] += lax.dot_general(last, right, NT, preferred_element_type=F32)
            field = jnp.where(same & (iota((128, width), 0) < 32), part[4:5], 0.0).astype(BF16)
            acc6[...] += lax.dot_general(last, field, NT, preferred_element_type=F32)
        code = (owner * 8 + rank).astype(F32)
        own = jnp.where(iota((TABLES, width), 0) == group, code, 0.0).astype(BF16)
        spot = jnp.where(
            (iota((128, width), 0) & 63) == (iota((128, width), 1) & 63), 1.0, 0.0
        ).astype(BF16)
        acc7[...] += lax.dot_general(own, spot, NT, preferred_element_type=F32)
        return carry

    lax.fori_loop(0, owner_ref.shape[1] // width, chunk, 0)
    msg_ref[pl.ds(5, TABLES, stride=8), :] = acc5[...]
    msg_ref[pl.ds(6, TABLES, stride=8), :] = acc6[...]
    msg_ref[pl.ds(7, TABLES, stride=8), :] = acc7[...]


def enter(me_t, me_s, with_partner):
    barrier = pltpu.get_barrier_semaphore()

    def greet(step, carry):
        pl.semaphore_signal(
            barrier, inc=1, device_id=(lax.rem(me_t + step, TABLES), me_s), device_id_type=MESH
        )
        return carry

    lax.fori_loop(1, TABLES, greet, 0)
    for step in range(1, YS):
        pl.semaphore_signal(
            barrier, inc=1, device_id=(me_t, lax.rem(me_s + 2 * step, 2 * YS)), device_id_type=MESH
        )
    if with_partner:
        core = lax.rem(me_s, 2)
        pl.semaphore_signal(
            barrier, inc=1, device_id=(me_t, me_s + 1 - 2 * core), device_id_type=MESH
        )
    pl.semaphore_wait(barrier, TABLES - 1 + YS - 1 + (1 if with_partner else 0))


def far_and_near(body):
    def pair(step, carry):
        body(step)
        body(TABLES - step)
        return carry

    lax.fori_loop(1, TABLES // 2, pair, 0)
    body(TABLES // 2)


def exchange_kernel(
    msg_ref, table_ref, got_ref, all_ref, other_ref, local_sem, swap_sem, row_sem, y_send, y_recv
):
    me_t, me_s = lax.axis_index("table"), lax.axis_index("scal")
    core = lax.rem(me_s, 2)
    me_y = lax.div(me_s, 2)
    partner = (me_t, me_s + 1 - 2 * core)
    enter(me_t, me_s, True)
    swap = pltpu.make_async_remote_copy(
        table_ref, other_ref, swap_sem.at[0], swap_sem.at[1], device_id=partner, device_id_type=MESH
    )

    def send(step):
        to = lax.rem(me_t + step, TABLES)
        pltpu.make_async_remote_copy(
            msg_ref.at[to], got_ref.at[me_t], row_sem.at[0], row_sem.at[1],
            device_id=(to, me_s), device_id_type=MESH,
        ).start()

    far_and_near(send)
    own = pltpu.make_async_copy(msg_ref.at[me_t], got_ref.at[me_t], local_sem.at[0])
    own.start()
    swap.start()
    own.wait()
    whole = pltpu.make_async_remote_copy(
        msg_ref.at[pl.ds(0, TABLES - 1)], got_ref.at[pl.ds(0, TABLES - 1)],
        row_sem.at[0], row_sem.at[1], device_id=partner, device_id_type=MESH,
    )
    whole.wait_recv()
    copies = []
    for step in range(1, YS):
        to = lax.rem(me_s + 2 * step, 2 * YS)
        copy = pltpu.make_async_remote_copy(
            got_ref, all_ref.at[me_y], y_send.at[step - 1], y_recv.at[step - 1],
            device_id=(me_t, to), device_id_type=MESH,
        )
        copy.start()
        copies.append(copy)
    keep = pltpu.make_async_copy(got_ref, all_ref.at[me_y], local_sem.at[1])
    keep.start()
    whole.wait_send()
    keep.wait()
    for copy in copies:
        copy.wait()
    swap.wait()


def slot_weights(tile, spread):
    tail = tile[5:6]
    f = [
        jnp.concatenate([tile[1 + n : 2 + n], extra], axis=1)
        for n, extra in enumerate(
            (pltpu.roll(tail, 96, 1), pltpu.roll(tail, 64, 1), pltpu.roll(tail, 32, 1), tile[6:7])
        )
    ]
    last = f[3]
    square = last * last
    cube = square * last
    remain = 1.0 - last
    cubic = (
        remain * remain * remain * (1.0 / 6.0),
        (3.0 * cube - 6.0 * square + 4.0) * (1.0 / 6.0),
        (-3.0 * cube + 3.0 * square + 3.0 * last + 1.0) * (1.0 / 6.0),
        cube * (1.0 / 6.0),
    )
    sub = iota((8, 256), 0)
    d = sub & 3
    inner = jnp.where(
        d < 2, jnp.where(d == 0, cubic[0], cubic[1]), jnp.where(d == 2, cubic[2], cubic[3])
    ) * jnp.where(sub < 4, 1.0 - f[2], f[2])
    first, second = (1.0 - f[0], f[0]), (1.0 - f[1], f[1])
    weight = jnp.concatenate([(one * two) * inner for one in first for two in second], axis=0)
    high = weight.astype(BF16)
    parts = jnp.concatenate([high, (weight - high.astype(F32)).astype(BF16)], axis=0)
    return lax.dot_general(parts[:, : 32 * MOST], spread, TN, preferred_element_type=F32)


def lookup_kernel(idx_ref, req_ref, near_ref, far_ref, out_ref, near, far, table, rows, wide, acc, pick, sem):
    bins = near_ref.shape[0]
    loads = [
        pltpu.make_async_copy(near_ref, near, sem.at[0]),
        pltpu.make_async_copy(far_ref, far, sem.at[1]),
    ]
    for load in loads:
        load.start()
    core = lax.rem(lax.axis_index("scal"), 2)
    slots = 32 * MOST
    k, lane = iota((256, 128), 0), iota((256, 128), 1)
    half = jnp.where((k >> 7) == 0, core, 1 - core)
    shifted = lane - (half * 4 + ((k >> 5) & 3))

    def choose(b, carry):
        pick[b] = jnp.where(shifted == 8 * b, 1.0, 0.0).astype(BF16)
        return carry

    lax.fori_loop(0, 16, choose, 0)
    for load in loads:
        load.wait()

    def weave(step, carry):
        for part in range(8):
            at = pl.multiple_of(step * 64 + part * 8, 8)
            table[pl.ds(2 * at + 8, 8, stride=2), :] = near[pl.ds(at, 8), :]
            table[pl.ds(2 * at + 9, 8, stride=2), :] = far[pl.ds(at, 8), :]
        return carry

    lax.fori_loop(0, bins // 64, weave, 0)
    spread = jnp.where((iota((64, 128), 0) & 31) == (iota((64, 128), 1) & 31), 1.0, 0.0).astype(BF16)

    pair_of = iota((8, 128), 0) >> 1

    def fetch(blk, slot):
        for at in range(0, slots, 4):
            group = None
            for r in range(4):
                row = idx_ref[2 * blk + ((at + r) // 128), (at + r) % 128]
                piece = table[pl.ds(row + (8 - 2 * r), 8), :]
                group = piece if r == 0 else jnp.where(pair_of == r, piece, group)
            rows[slot, 2 * at : 2 * at + 8, :] = group
        wide[slot] = slot_weights(req_ref[blk], spread)

    def contract(b, slot):
        left = rows[slot, pl.ds(0, slots, stride=2), :] * wide[slot]
        right = rows[slot, pl.ds(1, slots, stride=2), :] * wide[slot]
        left_hi, right_hi = left.astype(BF16), right.astype(BF16)
        left_lo = (left - left_hi.astype(F32)).astype(BF16)
        right_lo = (right - right_hi.astype(F32)).astype(BF16)
        chosen = pick[b]
        return jnp.dot(
            jnp.concatenate([left_hi, right_hi], axis=1), chosen, preferred_element_type=F32
        ) + jnp.dot(jnp.concatenate([left_lo, right_lo], axis=1), chosen, preferred_element_type=F32)

    def section(step, carry):
        acc[...] = jnp.zeros_like(acc)

        def four(j, base):
            b = 4 * j
            blk = base + b
            fetch(blk + 2, 2)
            fetch(blk + 3, 3)
            acc[...] += contract(b, 0) + contract(b + 1, 1)
            fetch(jnp.minimum(blk + 4, 2 * YS * 16 - 1), 0)
            fetch(jnp.minimum(blk + 5, 2 * YS * 16 - 1), 1)
            acc[...] += contract(b + 2, 2) + contract(b + 3, 3)
            return base

        lax.fori_loop(0, 4, four, step * 16)
        y, half_t = step // 2, lax.rem(step, 2)
        for q in range(MOST):
            for g in range(32):
                out_ref[y, g, half_t, q : q + 1, :] = acc[q * 32 + g : q * 32 + g + 1, :]
        return carry

    fetch(0, 0)
    fetch(1, 1)
    lax.fori_loop(0, 2 * YS, section, 0)


def reply_kernel(out_ref, got_ref, mid_ref, y_send, y_recv, row_sem, local_sem):
    me_t, me_s = lax.axis_index("table"), lax.axis_index("scal")
    me_y = lax.div(me_s, 2)
    enter(me_t, me_s, False)
    copies = []
    for step in range(1, YS):
        to_y = lax.rem(me_y + step, YS)
        copy = pltpu.make_async_remote_copy(
            out_ref.at[to_y], mid_ref.at[me_y], y_send.at[step - 1], y_recv.at[step - 1],
            device_id=(me_t, lax.rem(me_s + 2 * step, 2 * YS)), device_id_type=MESH,
        )
        copy.start()
        copies.append(copy)

    def pass_on(source, y):
        def send(step):
            to = lax.rem(me_t + step, TABLES)
            pltpu.make_async_remote_copy(
                source.at[to], got_ref.at[me_t, y], row_sem.at[0], row_sem.at[1],
                device_id=(to, me_s), device_id_type=MESH,
            ).start()

        far_and_near(send)

    keeps = [pltpu.make_async_copy(out_ref.at[me_y, me_t], got_ref.at[me_t, me_y], local_sem.at[0])]
    keeps[0].start()
    pass_on(out_ref.at[me_y], me_y)
    for step in range(1, YS):
        copies[step - 1].wait_recv()
        y = lax.rem(me_y + YS - step, YS)
        pass_on(mid_ref.at[y], y)
        keep = pltpu.make_async_copy(mid_ref.at[y, me_t], got_ref.at[me_t, y], local_sem.at[step])
        keep.start()
        keeps.append(keep)
    for keep in keeps:
        keep.wait()
    for copy in copies:
        copy.wait_send()
    whole = pltpu.make_async_remote_copy(
        got_ref.at[pl.ds(0, TABLES - 1)], got_ref.at[pl.ds(0, TABLES - 1)],
        row_sem.at[0], row_sem.at[1],
        device_id=(me_t, lax.rem(me_s + 2, 2 * YS)), device_id_type=MESH,
    )
    whole.wait_send()
    whole.wait_recv()


def filter_kernel(got_ref, code_ref, ops_ref, fil_ref, grad_ref, flat, turned, pencil):
    for y in range(YS):
        for half_t in range(2):
            at = 2 * y + half_t
            for o in range(TABLES):
                flat[at, o * 8 : o * 8 + MOST, :] = got_ref[o, y, half_t]
            turned[at] = flat[at].T

    lane = iota((8, 128), 1)

    def cells_of(at, t, b):
        code = jnp.broadcast_to(code_ref[t, 7:8, :].astype(I32), (8, 128))
        low = code & 127
        near = jnp.take_along_axis(turned[at, b * 8 : b * 8 + 8, 0:128], low, axis=1)
        far = jnp.take_along_axis(turned[at, b * 8 : b * 8 + 8, 128:256], low, axis=1)
        return jnp.where(code < 128, near, far)

    for half_t in range(2):
        for y in range(YS):
            at = 2 * y + half_t
            tiles = [
                jnp.where(
                    lane < 64, cells_of(at, half_t * 16 + b, b), cells_of(at, half_t * 16 + b + 8, b + 8)
                )
                for b in range(8)
            ]
            for bit in (1, 2, 4):
                keep = ((lane >> 3) & bit) == 0
                for i in range(8):
                    if not i & bit:
                        one, two = tiles[i], tiles[i + bit]
                        tiles[i] = jnp.where(keep, one, pltpu.roll(two, 8 * bit, 1))
                        tiles[i + bit] = jnp.where(keep, pltpu.roll(one, 128 - 8 * bit, 1), two)
            for r in range(8):
                pencil[half_t, pl.ds(y * 64 + r, 8, stride=8), :] = tiles[r]

    values = jnp.concatenate([pencil[0], pencil[1]], axis=1)
    fil_ref[...] = jnp.dot(
        values, ops_ref[:, 0:256], precision=lax.Precision.HIGHEST, preferred_element_type=F32
    )
    grad_ref[...] = jnp.dot(
        values, ops_ref[:, 256:512], precision=lax.Precision.HIGHEST, preferred_element_type=F32
    )


def on_device(cell_coords, flamelet_table, owner_shard, local_bin):
    cells = cell_coords.shape[1]
    bins = flamelet_table.shape[0]
    dma = pltpu.SemaphoreType.DMA
    vmem = pl.BlockSpec(memory_space=pltpu.VMEM)
    anywhere = pl.BlockSpec(memory_space=pl.ANY)
    shape = jax.ShapeDtypeStruct
    msg = pl.pallas_call(
        request_kernel,
        out_shape=shape((TABLES * 8, 128), F32),
        in_specs=[vmem] * 3,
        out_specs=vmem,
        scratch_shapes=[
            pltpu.VMEM((8, cells), F32),
            pltpu.VMEM((TABLES, 128), F32),
            pltpu.VMEM((TABLES, 128), F32),
            pltpu.VMEM((TABLES, 128), F32),
        ],
        name="build_requests",
    )(cell_coords, owner_shard.T, local_bin.reshape(1, cells))
    got, everything, other = pl.pallas_call(
        exchange_kernel,
        out_shape=(
            shape((TABLES, 8, 128), F32),
            shape((YS, TABLES, 8, 128), F32),
            shape((bins, 128), F32),
        ),
        in_specs=[anywhere] * 2,
        out_specs=(anywhere,) * 3,
        scratch_shapes=[dma((2,)), dma((2,)), dma((2,)), dma((YS - 1,)), dma((YS - 1,))],
        compiler_params=pltpu.CompilerParams(collective_id=0, has_side_effects=True),
        name="exchange_requests",
    )(msg.reshape(TABLES, 8, 128), flamelet_table)
    rows = everything.reshape(YS * TABLES, 8, 128)
    index = jnp.stack([rows[:, 0], rows[:, 5]], axis=1).astype(I32).reshape(2 * YS * TABLES, 128) * 2
    out = pl.pallas_call(
        lookup_kernel,
        out_shape=shape((YS, TABLES, 2, MOST, 128), F32),
        in_specs=[pl.BlockSpec(memory_space=pltpu.SMEM), vmem, anywhere, anywhere],
        out_specs=vmem,
        scratch_shapes=[
            pltpu.VMEM((bins, 128), F32),
            pltpu.VMEM((bins, 128), F32),
            pltpu.VMEM((2 * bins + 16, 128), F32),
            pltpu.VMEM((4, 2 * 32 * MOST, 128), F32),
            pltpu.VMEM((4, 32 * MOST, 128), F32),
            pltpu.VMEM((32 * MOST, 128), F32),
            pltpu.VMEM((16, 256, 128), BF16),
            dma((2,)),
        ],
        name="look_up",
    )(index, rows, flamelet_table, other)
    back, _ = pl.pallas_call(
        reply_kernel,
        out_shape=(
            shape((TABLES, YS, 2, MOST, 128), F32),
            shape((YS, TABLES, 2, MOST, 128), F32),
        ),
        in_specs=[anywhere],
        out_specs=(anywhere,) * 2,
        scratch_shapes=[dma((YS - 1,)), dma((YS - 1,)), dma((2,)), dma((YS,))],
        compiler_params=pltpu.CompilerParams(collective_id=1, has_side_effects=True),
        name="send_replies",
    )(out)
    length = 8 * TABLES
    filter_op = filter_table(length)
    ops = np.concatenate([filter_op.T, (derivative_table(length) @ filter_op).T], axis=1)
    filtered, gradient = pl.pallas_call(
        filter_kernel,
        out_shape=(shape((256, length), F32), shape((256, length), F32)),
        in_specs=[vmem] * 3,
        out_specs=(vmem,) * 2,
        scratch_shapes=[
            pltpu.VMEM((2 * YS, 256, 128), F32),
            pltpu.VMEM((2 * YS, 128, 256), F32),
            pltpu.VMEM((2, 256, 128), F32),
        ],
        name="place_and_filter",
    )(back, got, jnp.asarray(ops.astype(np.float32)))
    return filtered.reshape(32, 8, length), gradient.reshape(32, 8, length)


def solution(mesh):
    return jax.shard_map(
        on_device,
        mesh=mesh,
        in_specs=(
            P(None, ("table", "scal")),
            P("table", "scal"),
            P(("table", "scal"), None),
            P(("table", "scal")),
        ),
        out_specs=(P(None, ("table", "scal"), None), P(None, ("table", "scal"), None)),
        check_vma=False,
    )
```
